256 devices in a mesh: mp: 8 (over x, core), ctx: 32 (over z, y).
Axes of the slice: x: 4, y: 4, z: 8, core: 2. Of those that a mesh axis runs over, the one named last changes fastest.
Arguments:
- queries: bfloat16 [262144, 1024], P(('mp', 'ctx')), parts along dimension 0, may hold values from -6 to 6
- key_rows: bfloat16 [262144, 1024], P(('mp', 'ctx')), parts along dimension 0, may hold values from -6 to 6
- value_rows: bfloat16 [262144, 1024], P(('mp', 'ctx')), parts along dimension 0, may hold values from -6 to 6
- conv_weight: float32 [24, 4, 1024], P('mp'), parts along dimension 0, may hold values from -3 to 3
- head_gain: float32 [8192], P('mp'), parts along dimension 0, may hold values from 0.1 to 1.9
Outputs:
- attended: bfloat16 [262144, 1024], P(('mp', 'ctx')), parts along dimension 0
The draws below stay inside these ranges and needn't reach their ends.
There are 8 independent parts, one for each index of `mp`. The reference program is written for one: setup_inputs(seed, part) draws one part's arguments, and reference() takes and returns one part's arrays. A program takes and returns all parts, laid end to end along the dimension named above; each array names one. Nothing has to cross between parts.
All inputs are finite; a program needn't handle non-finite values.
Results may differ from the reference program's by a relative error of at most 0.006.
Values may be sent and summed in bfloat16 or wider, within the bound.
A program may use at most 128 MiB of HBM per device.

```python
import jax
import jax.numpy as jnp
from jax import lax

HEADS = 8
HDIM = 128
CONV = 4
TOK_DEV = 1024
HD = 1024
TOKENS = 32768
N_CTX = 32


def block_levels(stream_key, extent, cuts, low, top_value):
    loudness, own = 1.0, jax.random.fold_in(stream_key, 6)
    for dim, blocks in cuts:
        draws = jnp.exp(jax.random.uniform(jax.random.fold_in(own, dim), (blocks,), jnp.float32, low / len(cuts), top_value / len(cuts)))
        loudness = loudness * jnp.repeat(draws, extent[dim] // blocks).reshape([-1 if axis == dim else 1 for axis in range(len(extent))])
    return loudness


def bell_draw(own_key, extent, spread, bound, split=(), dtype=jnp.bfloat16):
    entries = spread * jax.random.normal(own_key, extent, jnp.float32)
    if split:
        entries = entries * block_levels(own_key, extent, split, -0.22, 0.18)
    return jnp.clip(entries, -bound, bound).astype(dtype)


def setup_inputs(seed: int = 0, part: int = 0) -> dict:
    arg_keys = jax.random.split(jax.random.key(seed), 6)
    part_keys = jax.random.split(jax.random.fold_in(arg_keys[5], part), 6)
    queries = bell_draw(part_keys[0], (TOKENS, HD), 1.0, 6.0, ((0, 32),))
    key_rows = bell_draw(part_keys[1], (TOKENS, HD), 1.0, 6.0, ((0, 32),))
    value_rows = bell_draw(part_keys[2], (TOKENS, HD), 1.0, 6.0, ((0, 32),))
    conv_weight = bell_draw(part_keys[3], (3, CONV, HD), 0.5, 3.0, (), jnp.float32)
    head_gain = jnp.clip(1.0 + 0.18 * jax.random.normal(part_keys[4], (HD,), jnp.float32), 0.1, 1.9)
    return dict(queries=queries, key_rows=key_rows, value_rows=value_rows, conv_weight=conv_weight, head_gain=head_gain)


def causal_conv(rows, taps):
    tokens_all = rows.shape[0]
    padded = jnp.concatenate([jnp.zeros((CONV - 1, rows.shape[1]), jnp.float32), rows.astype(jnp.float32)], axis=0)
    total = jnp.zeros((tokens_all, rows.shape[1]), jnp.float32)
    for tap in range(CONV):
        total = total + taps[tap][None, :] * padded[tap:tap + tokens_all]
    return total

def reference(queries, key_rows, value_rows, conv_weight, head_gain):
    query_f = (jax.nn.silu(causal_conv(queries, conv_weight[0])) * HDIM ** (-0.5)).astype(jnp.bfloat16)
    key_f = jax.nn.silu(causal_conv(key_rows, conv_weight[1])).astype(jnp.bfloat16)
    value_f = causal_conv(value_rows, conv_weight[2]).astype(jnp.bfloat16)
    query_b = query_f.reshape(N_CTX, TOK_DEV, HEADS, HDIM)
    key_b = key_f.reshape(N_CTX, TOK_DEV, HEADS, HDIM)
    value_b = value_f.reshape(N_CTX, TOK_DEV, HEADS, HDIM)
    causal = jnp.arange(TOK_DEV)[:, None] >= jnp.arange(TOK_DEV)[None, :]

    def block_step(state, pieces):
        query_p, key_p, value_p = pieces
        qq = query_p.astype(jnp.float32)
        kk = key_p.astype(jnp.float32)
        vv = value_p.astype(jnp.float32)
        scores = jnp.einsum('thd,shd->hts', qq, kk)
        scores = jnp.where(causal[None], scores, 0.0).astype(jnp.bfloat16)
        inner = jnp.einsum('hts,she->the', scores.astype(jnp.float32), vv)
        prefix = state.astype(jnp.bfloat16).astype(jnp.float32)
        cross = jnp.einsum('thd,hde->the', qq, prefix)
        local = jnp.einsum('shd,she->hde', kk, vv)
        return (state + local, inner + cross)
    start = jnp.zeros((HEADS, HDIM, HDIM), jnp.float32)
    final_state, outputs = lax.scan(block_step, start, (query_b, key_b, value_b))
    outputs = outputs.reshape(N_CTX * TOK_DEV, HEADS, HDIM)
    scale_inv = lax.rsqrt(lax.optimization_barrier(jnp.mean(outputs * outputs, axis=2, keepdims=True)) + 1e-06)
    normed = outputs * scale_inv * head_gain.reshape(HEADS, HDIM)[None]
    return normed.reshape(N_CTX * TOK_DEV, HEADS * HDIM).astype(jnp.bfloat16)
```

```python
import functools

import jax
import jax.numpy as jnp
from jax import lax
from jax.experimental import pallas as pl
from jax.experimental.pallas import tpu as pltpu
from jax.sharding import PartitionSpec as P

HDIM = 128
CONV = 4
PAD = 16
CHUNK = 256
MESH = pl.DeviceIdType.MESH


def conv_half(rows_ref, weights, chunk, lanes):
    rows = rows_ref[pl.ds(pl.multiple_of(chunk * CHUNK, CHUNK), CHUNK + PAD), lanes].astype(jnp.float32)
    back1 = pltpu.roll(rows, 1, 0)
    late = weights[3] * rows + weights[2] * back1
    early = weights[1] * rows + weights[0] * back1
    return (late + pltpu.roll(early, 2, 0))[PAD:]


def kernel(
    n, heads, tokens,
    q_hbm, k_hbm, v_hbm, w_hbm, g_hbm, out_hbm,
    q_raw, k_raw, v_raw, w_ref, g_ref, q_feat, k_feat, v_feat,
    inner, states, send1, land1, send2, land2, out_buf,
    load_sems, halo_send, halo_recv, send1_sems, recv1_sems, send2_sems, recv2_sems, out_sems,
):
    me = lax.axis_index("ctx")
    chunks = tokens // CHUNK
    piece = heads * HDIM // n
    per_head = HDIM // piece
    raws, hbms = (q_raw, k_raw, v_raw), (q_hbm, k_hbm, v_hbm)

    barrier = pltpu.get_barrier_semaphore()
    for step in range(1, n):
        pl.semaphore_signal(barrier, inc=1, device_id={"ctx": lax.rem(me + step, n)}, device_id_type=MESH)

    small = [
        pltpu.make_async_copy(w_hbm, w_ref, load_sems.at[3 * chunks]),
        pltpu.make_async_copy(g_hbm, g_ref, load_sems.at[3 * chunks + 1]),
    ]
    loads = {}
    for kind in range(3):
        for chunk in range(chunks):
            loads[kind, chunk] = pltpu.make_async_copy(
                hbms[kind].at[pl.ds(chunk * CHUNK, CHUNK)],
                raws[kind].at[pl.ds(PAD + chunk * CHUNK, CHUNK)],
                load_sems.at[kind * chunks + chunk],
            )
    small[0].start()
    for chunk in reversed(range(chunks)):
        loads[1, chunk].start()
        loads[2, chunk].start()
    small[1].start()
    for chunk in reversed(range(chunks)):
        loads[0, chunk].start()

    @pl.when(me == 0)
    def _():
        for raw in raws:
            raw[0:PAD] = jnp.zeros((PAD, raw.shape[1]), raw.dtype)

    small[0].wait()

    def halo(kind):
        return pltpu.make_async_remote_copy(
            src_ref=hbms[kind].at[pl.ds(tokens - 8, 8)],
            dst_ref=raws[kind].at[pl.ds(PAD - 8, 8)],
            send_sem=halo_send.at[kind],
            recv_sem=halo_recv.at[kind],
            device_id={"ctx": lax.rem(me + 1, n)},
            device_id_type=MESH,
        )

    def key_value(chunk):
        @pl.loop(0, heads)
        def _(head):
            lanes = pl.ds(pl.multiple_of(head * HDIM, HDIM), HDIM)
            half = conv_half(k_raw, [w_ref[1, tap : tap + 1, lanes] * 0.5 for tap in range(CONV)], chunk, lanes)
            key = (half + half * jnp.tanh(half)).astype(jnp.bfloat16)
            value = conv_half(v_raw, [w_ref[2, tap : tap + 1, lanes] for tap in range(CONV)], chunk, lanes).astype(jnp.bfloat16)
            k_feat[head, chunk] = key
            v_feat[head, chunk] = value
            states[chunk, head] = lax.dot_general(
                key, value, (((0,), (0,)), ((), ())), preferred_element_type=jnp.float32
            )

    for chunk in reversed(range(1, chunks)):
        if chunk == chunks - 1:
            loads[1, chunk].wait()
            loads[2, chunk].wait()
        loads[1, chunk - 1].wait()
        loads[2, chunk - 1].wait()
        key_value(chunk)

    pl.semaphore_wait(barrier, n - 1)

    @pl.when(me < n - 1)
    def _():
        for kind in (1, 2, 0):
            halo(kind).start()

    @pl.when(me > 0)
    def _():
        halo(1).wait_recv()
        halo(2).wait_recv()

    key_value(0)

    @pl.loop(0, heads)
    def _(head):
        total = states[0, head]
        for chunk in range(1, chunks):
            own = states[chunk, head]
            states[chunk, head] = total
            total = total + own
        send1[pl.ds(head * per_head, per_head)] = total.astype(jnp.bfloat16).reshape(per_head, piece, HDIM)

    def give(step):
        peer = lax.rem(me + step, n)
        return pltpu.make_async_remote_copy(
            src_ref=send1.at[peer], dst_ref=land1.at[me], send_sem=send1_sems.at[step], recv_sem=recv1_sems.at[me],
            device_id={"ctx": peer}, device_id_type=MESH,
        )

    def given(step):
        peer = lax.rem(me + n - step, n)
        return pltpu.make_async_remote_copy(
            src_ref=send1.at[peer], dst_ref=land1.at[peer], send_sem=send1_sems.at[step], recv_sem=recv1_sems.at[peer],
            device_id={"ctx": peer}, device_id_type=MESH,
        )

    def reply(step):
        peer = lax.rem(me + step, n)
        return pltpu.make_async_remote_copy(
            src_ref=send2.at[peer], dst_ref=land2.at[me], send_sem=send2_sems.at[step], recv_sem=recv2_sems.at[me],
            device_id={"ctx": peer}, device_id_type=MESH,
        )

    def replied(step):
        peer = lax.rem(me + n - step, n)
        return pltpu.make_async_remote_copy(
            src_ref=send2.at[peer], dst_ref=land2.at[peer], send_sem=send2_sems.at[step], recv_sem=recv2_sems.at[peer],
            device_id={"ctx": peer}, device_id_type=MESH,
        )

    order = sorted(range(1, n), key=lambda step: -min(step, n - step))
    for step in order:
        give(step).start()
    land1[me] = send1[me]

    small[1].wait()
    for chunk in range(chunks):
        loads[0, chunk].wait()

    @pl.when(me > 0)
    def _():
        halo(0).wait_recv()

    def query(chunk):
        @pl.loop(0, heads)
        def _(head):
            lanes = pl.ds(pl.multiple_of(head * HDIM, HDIM), HDIM)
            half = conv_half(q_raw, [w_ref[0, tap : tap + 1, lanes] * 0.5 for tap in range(CONV)], chunk, lanes)
            feat = ((half + half * jnp.tanh(half)) * HDIM ** (-0.5)).astype(jnp.bfloat16)
            q_feat[head, chunk] = feat
            scores = lax.dot_general(
                feat, k_feat[head, chunk], (((1,), (1,)), ((), ())), preferred_element_type=jnp.float32
            )
            row = lax.broadcasted_iota(jnp.int32, scores.shape, 0)
            col = lax.broadcasted_iota(jnp.int32, scores.shape, 1)
            scores = jnp.where(row >= col, scores, 0.0).astype(jnp.bfloat16)
            inner[head, chunk] = jnp.dot(scores, v_feat[head, chunk], preferred_element_type=jnp.float32)

    query(0)
    query(1)
    for step in order:
        given(step).wait_recv()
    total = jnp.zeros((piece, HDIM), jnp.float32)
    for block in range(n):
        send2[block] = total.astype(jnp.bfloat16)
        total = total + land1[block].astype(jnp.float32)
    for step in order:
        reply(step).start()
    land2[me] = send2[me]
    query(2)
    query(3)
    for step in order:
        replied(step).wait_recv()

    def finish(chunk):
        @pl.loop(0, heads)
        def _(head):
            lanes = pl.ds(pl.multiple_of(head * HDIM, HDIM), HDIM)
            prefix = land2[pl.ds(head * per_head, per_head)].reshape(HDIM, HDIM)
            if chunk:
                prefix = (prefix.astype(jnp.float32) + states[chunk, head]).astype(jnp.bfloat16)
            outputs = inner[head, chunk] + jnp.dot(q_feat[head, chunk], prefix, preferred_element_type=jnp.float32)
            scale_inv = lax.rsqrt(jnp.mean(outputs * outputs, axis=1, keepdims=True) + 1e-06)
            out_buf[pl.ds(chunk * CHUNK, CHUNK), lanes] = (outputs * scale_inv * g_ref[0:1, lanes]).astype(jnp.bfloat16)

        return pltpu.make_async_copy(
            out_buf.at[pl.ds(chunk * CHUNK, CHUNK)], out_hbm.at[pl.ds(chunk * CHUNK, CHUNK)], out_sems.at[chunk]
        )

    stores = []
    for chunk in range(chunks):
        store = finish(chunk)
        store.start()
        stores.append(store)

    @pl.when(me < n - 1)
    def _():
        for kind in range(3):
            halo(kind).wait_send()

    for step in order:
        give(step).wait_send()
        reply(step).wait_send()
    for store in stores:
        store.wait()


def body(queries, key_rows, value_rows, conv_weight, head_gain):
    tokens, width = queries.shape
    heads = width // HDIM
    n = lax.axis_size("ctx")
    chunks = tokens // CHUNK
    piece = heads * HDIM // n
    anywhere = pl.BlockSpec(memory_space=pl.ANY)
    bf16, f32 = jnp.bfloat16, jnp.float32
    dma = pltpu.SemaphoreType.DMA
    return pl.pallas_call(
        functools.partial(kernel, n, heads, tokens),
        out_shape=jax.ShapeDtypeStruct((tokens, width), bf16),
        in_specs=[anywhere] * 5,
        out_specs=anywhere,
        scratch_shapes=[
            *[pltpu.VMEM((tokens + PAD, width), bf16)] * 3,
            pltpu.VMEM((3, CONV, width), f32),
            pltpu.VMEM((1, width), f32),
            *[pltpu.VMEM((heads, chunks, CHUNK, HDIM), bf16)] * 3,
            pltpu.VMEM((heads, chunks, CHUNK, HDIM), f32),
            pltpu.VMEM((chunks, heads, HDIM, HDIM), f32),
            *[pltpu.VMEM((n, piece, HDIM), bf16)] * 4,
            pltpu.VMEM((tokens, width), bf16),
            dma((3 * chunks + 2,)), dma((3,)), dma((3,)),
            dma((n,)), dma((n,)), dma((n,)), dma((n,)),
            dma((chunks,)),
        ],
        compiler_params=pltpu.CompilerParams(
            collective_id=0, has_side_effects=True, vmem_limit_bytes=48 * 1024 * 1024
        ),
        name="linear_attention",
    )(queries, key_rows, value_rows, conv_weight, head_gain.reshape(1, width))


def solution(mesh):
    return jax.shard_map(
        body,
        mesh=mesh,
        in_specs=(
            P(("mp", "ctx"), None),
            P(("mp", "ctx"), None),
            P(("mp", "ctx"), None),
            P("mp", None, None),
            P("mp"),
        ),
        out_specs=P(("mp", "ctx"), None),
        check_vma=False,
    )
```

```python
import functools

import jax
import jax.numpy as jnp
from jax import lax
from jax.experimental import pallas as pl
from jax.experimental.pallas import tpu as pltpu
from jax.sharding import PartitionSpec as P

HDIM = 128
CONV = 4
PAD = 16
CHUNK = 256
KV_WIDE, Q_WIDE, OUT_WIDE = 4, 4, 4
MESH = pl.DeviceIdType.MESH


def conv(rows_ref, wide, weights, chunk, lanes):
    wide[...] = rows_ref[pl.ds(chunk * CHUNK, CHUNK + PAD), lanes].astype(jnp.float32)
    terms = [weights[tap] * wide[pl.ds(PAD - CONV + 1 + tap, CHUNK)] for tap in range(CONV)]
    return (terms[3] + terms[2]) + (terms[1] + terms[0])


def kernel(
    n, heads, tokens,
    q_hbm, k_hbm, v_hbm, w_hbm, g_hbm, out_hbm,
    q_raw, k_raw, v_raw, w_ref, g_ref, q_feat, k_feat, v_feat,
    inner, states, send1, land1, send2, land2, out_buf, wide,
    load_sems, halo_send, halo_recv, send1_sems, recv1_sems, send2_sems, recv2_sems, out_sems,
):
    me = lax.axis_index("ctx")
    chunks = tokens // CHUNK
    piece = heads * HDIM // n
    per_head = HDIM // piece
    raws, hbms = (q_raw, k_raw, v_raw), (q_hbm, k_hbm, v_hbm)

    barrier = pltpu.get_barrier_semaphore()
    for step in range(1, n):
        pl.semaphore_signal(barrier, inc=1, device_id={"ctx": lax.rem(me + step, n)}, device_id_type=MESH)

    small = [
        pltpu.make_async_copy(w_hbm, w_ref, load_sems.at[3 * chunks]),
        pltpu.make_async_copy(g_hbm, g_ref, load_sems.at[3 * chunks + 1]),
    ]
    loads = {}
    for kind in range(3):
        for chunk in range(chunks):
            loads[kind, chunk] = pltpu.make_async_copy(
                hbms[kind].at[pl.ds(chunk * CHUNK, CHUNK)],
                raws[kind].at[pl.ds(PAD + chunk * CHUNK, CHUNK)],
                load_sems.at[kind * chunks + chunk],
            )
    small[0].start()
    for chunk in reversed(range(chunks)):
        loads[1, chunk].start()
        loads[2, chunk].start()
    small[1].start()
    for chunk in reversed(range(chunks)):
        loads[0, chunk].start()

    @pl.when(me == 0)
    def _():
        for raw in raws:
            raw[0:PAD] = jnp.zeros((PAD, raw.shape[1]), raw.dtype)

    small[0].wait()

    def halo(kind):
        return pltpu.make_async_remote_copy(
            src_ref=hbms[kind].at[pl.ds(tokens - 8, 8)],
            dst_ref=raws[kind].at[pl.ds(PAD - 8, 8)],
            send_sem=halo_send.at[kind],
            recv_sem=halo_recv.at[kind],
            device_id={"ctx": lax.rem(me + 1, n)},
            device_id_type=MESH,
        )

    def several(count, width, one):
        @pl.loop(0, count // width)
        def _(turn):
            for slot in range(width):
                one(turn * width + slot, slot)

    def lanes_of(head):
        return pl.ds(pl.multiple_of(head * HDIM, HDIM), HDIM)

    def key_value(chunk):
        def one(head, slot):
            lanes = lanes_of(head)
            half = conv(k_raw, wide.at[2 * slot], [w_ref[1, tap : tap + 1, lanes] * 0.5 for tap in range(CONV)], chunk, lanes)
            key = (half + half * jnp.tanh(half)).astype(jnp.bfloat16)
            taps = [w_ref[2, tap : tap + 1, lanes] for tap in range(CONV)]
            value = conv(v_raw, wide.at[2 * slot + 1], taps, chunk, lanes).astype(jnp.bfloat16)
            k_feat[head, chunk] = key
            v_feat[head, chunk] = value
            states[chunk, head] = lax.dot_general(
                key, value, (((0,), (0,)), ((), ())), preferred_element_type=jnp.float32
            )

        several(heads, KV_WIDE, one)

    for chunk in reversed(range(1, chunks)):
        if chunk == chunks - 1:
            loads[1, chunk].wait()
            loads[2, chunk].wait()
        loads[1, chunk - 1].wait()
        loads[2, chunk - 1].wait()
        key_value(chunk)

    pl.semaphore_wait(barrier, n - 1)

    @pl.when(me < n - 1)
    def _():
        for kind in (1, 2, 0):
            halo(kind).start()

    @pl.when(me > 0)
    def _():
        halo(1).wait_recv()
        halo(2).wait_recv()

    key_value(0)

    @pl.loop(0, heads)
    def _(head):
        total = states[0, head]
        for chunk in range(1, chunks):
            own = states[chunk, head]
            states[chunk, head] = total
            total = total + own
        send1[pl.ds(head * per_head, per_head)] = total.astype(jnp.bfloat16).reshape(per_head, piece, HDIM)

    def give(step):
        peer = lax.rem(me + step, n)
        return pltpu.make_async_remote_copy(
            src_ref=send1.at[peer], dst_ref=land1.at[me], send_sem=send1_sems.at[step], recv_sem=recv1_sems.at[me],
            device_id={"ctx": peer}, device_id_type=MESH,
        )

    def given(step):
        peer = lax.rem(me + n - step, n)
        return pltpu.make_async_remote_copy(
            src_ref=send1.at[peer], dst_ref=land1.at[peer], send_sem=send1_sems.at[step], recv_sem=recv1_sems.at[peer],
            device_id={"ctx": peer}, device_id_type=MESH,
        )

    def reply(step):
        peer = lax.rem(me + step, n)
        return pltpu.make_async_remote_copy(
            src_ref=send2.at[peer], dst_ref=land2.at[me], send_sem=send2_sems.at[step], recv_sem=recv2_sems.at[me],
            device_id={"ctx": peer}, device_id_type=MESH,
        )

    def replied(step):
        peer = lax.rem(me + n - step, n)
        return pltpu.make_async_remote_copy(
            src_ref=send2.at[peer], dst_ref=land2.at[peer], send_sem=send2_sems.at[step], recv_sem=recv2_sems.at[peer],
            device_id={"ctx": peer}, device_id_type=MESH,
        )

    order = sorted(range(1, n), key=lambda step: -min(step, n - step))
    for step in order:
        give(step).start()
    land1[me] = send1[me]

    small[1].wait()
    for chunk in range(chunks):
        loads[0, chunk].wait()

    @pl.when(me > 0)
    def _():
        halo(0).wait_recv()

    def query(chunk):
        def one(head, slot):
            lanes = lanes_of(head)
            half = conv(q_raw, wide.at[slot], [w_ref[0, tap : tap + 1, lanes] * 0.5 for tap in range(CONV)], chunk, lanes)
            feat = ((half + half * jnp.tanh(half)) * HDIM ** (-0.5)).astype(jnp.bfloat16)
            q_feat[head, chunk] = feat
            scores = lax.dot_general(
                feat, k_feat[head, chunk], (((1,), (1,)), ((), ())), preferred_element_type=jnp.float32
            )
            row = lax.broadcasted_iota(jnp.int32, scores.shape, 0)
            col = lax.broadcasted_iota(jnp.int32, scores.shape, 1)
            scores = jnp.where(row >= col, scores, 0.0).astype(jnp.bfloat16)
            inner[head, chunk] = jnp.dot(scores, v_feat[head, chunk], preferred_element_type=jnp.float32)

        several(heads, Q_WIDE, one)

    query(0)
    query(1)
    for step in order:
        given(step).wait_recv()
    total = jnp.zeros((piece, HDIM), jnp.float32)
    for block in range(n):
        send2[block] = total.astype(jnp.bfloat16)
        total = total + land1[block].astype(jnp.float32)
    for step in order:
        reply(step).start()
    land2[me] = send2[me]
    query(2)
    query(3)
    for step in order:
        replied(step).wait_recv()

    def finish(chunk):
        def one(head, slot):
            lanes = lanes_of(head)
            prefix = land2[pl.ds(head * per_head, per_head)].reshape(HDIM, HDIM)
            if chunk:
                prefix = (prefix.astype(jnp.float32) + states[chunk, head]).astype(jnp.bfloat16)
            outputs = inner[head, chunk] + jnp.dot(q_feat[head, chunk], prefix, preferred_element_type=jnp.float32)
            scale_inv = lax.rsqrt(jnp.mean(outputs * outputs, axis=1, keepdims=True) + 1e-06)
            out_buf[pl.ds(chunk * CHUNK, CHUNK), lanes] = (outputs * scale_inv * g_ref[0:1, lanes]).astype(jnp.bfloat16)

        several(heads, OUT_WIDE, one)
        return pltpu.make_async_copy(
            out_buf.at[pl.ds(chunk * CHUNK, CHUNK)], out_hbm.at[pl.ds(chunk * CHUNK, CHUNK)], out_sems.at[chunk]
        )

    stores = []
    for chunk in range(chunks):
        store = finish(chunk)
        store.start()
        stores.append(store)

    @pl.when(me < n - 1)
    def _():
        for kind in range(3):
            halo(kind).wait_send()

    for step in order:
        give(step).wait_send()
        reply(step).wait_send()
    for store in stores:
        store.wait()


def body(queries, key_rows, value_rows, conv_weight, head_gain):
    tokens, width = queries.shape
    heads = width // HDIM
    n = lax.axis_size("ctx")
    chunks = tokens // CHUNK
    piece = heads * HDIM // n
    anywhere = pl.BlockSpec(memory_space=pl.ANY)
    bf16, f32 = jnp.bfloat16, jnp.float32
    dma = pltpu.SemaphoreType.DMA
    return pl.pallas_call(
        functools.partial(kernel, n, heads, tokens),
        out_shape=jax.ShapeDtypeStruct((tokens, width), bf16),
        in_specs=[pl.BlockSpec(memory_space=pltpu.HBM)] * 5,
        out_specs=anywhere,
        scratch_shapes=[
            *[pltpu.VMEM((tokens + PAD, width), bf16)] * 3,
            pltpu.VMEM((3, CONV, width), f32),
            pltpu.VMEM((1, width), f32),
            *[pltpu.VMEM((heads, chunks, CHUNK, HDIM), bf16)] * 3,
            pltpu.VMEM((heads, chunks, CHUNK, HDIM), f32),
            pltpu.VMEM((chunks, heads, HDIM, HDIM), f32),
            *[pltpu.VMEM((n, piece, HDIM), bf16)] * 4,
            pltpu.VMEM((tokens, width), bf16),
            pltpu.VMEM((max(2 * KV_WIDE, Q_WIDE), CHUNK + PAD, HDIM), f32),
            dma((3 * chunks + 2,)), dma((3,)), dma((3,)),
            dma((n,)), dma((n,)), dma((n,)), dma((n,)),
            dma((chunks,)),
        ],
        compiler_params=pltpu.CompilerParams(
            collective_id=0, has_side_effects=True, vmem_limit_bytes=48 * 1024 * 1024
        ),
        name="linear_attention",
    )(*[pltpu.with_memory_space_constraint(x, pltpu.HBM) for x in (queries, key_rows, value_rows, conv_weight, head_gain.reshape(1, width))])


def solution(mesh):
    return jax.shard_map(
        body,
        mesh=mesh,
        in_specs=(
            P(("mp", "ctx"), None),
            P(("mp", "ctx"), None),
            P(("mp", "ctx"), None),
            P("mp", None, None),
            P("mp"),
        ),
        out_specs=P(("mp", "ctx"), None),
        check_vma=False,
    )
```

```python
import functools

import jax
import jax.numpy as jnp
from jax import lax
from jax.experimental import pallas as pl
from jax.experimental.pallas import tpu as pltpu
from jax.sharding import PartitionSpec as P

HDIM = 128
CONV = 4
PAD = 16
TAIL = 8
CHUNK = 256
MESH = pl.DeviceIdType.MESH


def conv(wide, weights, rows):
    terms = [weights[tap] * wide[pl.ds(PAD - CONV + 1 + tap, rows)] for tap in range(CONV)]
    return (terms[3] + terms[2]) + (terms[1] + terms[0])


def kernel(
    n, heads, tokens,
    q_hbm, k_hbm, v_hbm, w_hbm, g_hbm, out_hbm,
    q_raw, k_raw, v_raw, halo_k, halo_v, w_ref, g_ref, q_feat, k_feat, v_feat,
    inner, states, send1, land1, send2, land2, send3, land3, out_buf, wide,
    load_sems, halo_send, halo_recv, send1_sems, recv1_sems, send2_sems, recv2_sems, send3_sems, recv3_sems,
    ready_sems, out_sems,
):
    me = lax.axis_index("ctx")
    groups = n // heads
    group, member = me // heads, lax.rem(me, heads)
    chunks = tokens // CHUNK
    bf16, f32 = jnp.bfloat16, jnp.float32

    def mate(step):
        return group * heads + lax.rem(member + step, heads)

    barrier = pltpu.get_barrier_semaphore()

    def greet(peer):
        pl.semaphore_signal(barrier, inc=1, device_id={"ctx": peer}, device_id_type=MESH)

    for step in range(1, heads):
        greet(mate(step))
    for other in range(1, groups):
        @pl.when(group < other)
        def _():
            greet(other * heads + member)

    @pl.when(jnp.logical_and(member == 0, group > 0))
    def _():
        greet(me - 1)

    w_load = pltpu.make_async_copy(w_hbm, w_ref, load_sems.at[3, 0])
    g_load = pltpu.make_async_copy(g_hbm, g_ref, load_sems.at[3, 1])

    def load(kind, chunk):
        rows = chunk * CHUNK
        return pltpu.make_async_copy(
            (q_hbm, k_hbm, v_hbm)[kind].at[pl.ds(rows, CHUNK)],
            (q_raw, k_raw, v_raw)[kind].at[pl.ds(PAD + rows, CHUNK)],
            load_sems.at[kind, chunk],
        )

    w_load.start()
    for chunk in range(chunks):
        load(1, chunk).start()
        load(2, chunk).start()
    g_load.start()
    for chunk in range(chunks):
        load(0, chunk).start()

    k_raw[0:PAD] = jnp.zeros((PAD, heads * HDIM), bf16)
    v_raw[0:PAD] = jnp.zeros((PAD, heads * HDIM), bf16)

    @pl.when(me == 0)
    def _():
        q_raw[0:PAD] = jnp.zeros((PAD, heads * HDIM), bf16)
        halo_k[...] = jnp.zeros((TAIL, heads * HDIM), bf16)
        halo_v[...] = jnp.zeros((TAIL, heads * HDIM), bf16)

    for other in range(groups - 1):
        @pl.when(group <= other)
        def _():
            land3[other] = jnp.zeros((HDIM, HDIM), bf16)

    def halo(kind):
        return pltpu.make_async_remote_copy(
            src_ref=(q_hbm, k_hbm, v_hbm)[kind].at[pl.ds(tokens - TAIL, TAIL)],
            dst_ref=(q_raw.at[pl.ds(PAD - TAIL, TAIL)], halo_k, halo_v)[kind],
            send_sem=halo_send.at[kind],
            recv_sem=halo_recv.at[kind],
            device_id={"ctx": lax.rem(me + 1, n)},
            device_id_type=MESH,
        )

    def lanes_of(head):
        return pl.ds(head * HDIM, HDIM)

    def taps(kind, head, factor=None):
        weights = [w_ref[kind, tap : tap + 1, lanes_of(head)] for tap in range(CONV)]
        return weights if factor is None else [weight * factor for weight in weights]

    def silu(half):
        return half + half * jnp.tanh(half)

    def outer(key, value):
        return lax.dot_general(key, value, (((0,), (0,)), ((), ())), preferred_element_type=f32)

    w_load.wait()

    @pl.loop(0, chunks)
    def _(chunk):
        load(1, chunk).wait()
        load(2, chunk).wait()
        rows = pl.ds(pl.multiple_of(chunk * CHUNK, CHUNK), CHUNK + PAD)
        for head in range(heads):
            wide[2 * head] = k_raw[rows, lanes_of(head)].astype(f32)
            key = silu(conv(wide.at[2 * head], taps(1, head, 0.5), CHUNK)).astype(bf16)
            wide[2 * head + 1] = v_raw[rows, lanes_of(head)].astype(f32)
            value = conv(wide.at[2 * head + 1], taps(2, head), CHUNK).astype(bf16)
            k_feat[head, chunk] = key
            v_feat[head, chunk] = value
            states[chunk, head] = outer(key, value)

    waits = heads - 1 + group + jnp.logical_and(member == heads - 1, group < groups - 1).astype(jnp.int32)
    pl.semaphore_wait(barrier, waits)

    @pl.when(me < n - 1)
    def _():
        for kind in (1, 2, 0):
            halo(kind).start()

    for other in range(groups - 1):
        @pl.when(group > other)
        def _():
            pl.semaphore_signal(
                ready_sems.at[group], inc=1, device_id={"ctx": other * heads + member}, device_id_type=MESH
            )

    @pl.when(me > 0)
    def _():
        halo(1).wait_recv()
        halo(2).wait_recv()

    for head in range(heads):
        new = []
        for kind, raw, tail in ((1, k_raw, halo_k), (2, v_raw, halo_v)):
            slot = wide.at[2 * head + kind - 1]
            slot[PAD - TAIL : PAD] = tail[:, lanes_of(head)].astype(f32)
            slot[PAD : 2 * PAD] = raw[PAD : 2 * PAD, lanes_of(head)].astype(f32)
            new.append(conv(slot, taps(kind, head, 0.5 if kind == 1 else None), PAD))
        key, value = silu(new[0]).astype(bf16), new[1].astype(bf16)
        old_key, old_value = k_feat[head, 0, 0:PAD], v_feat[head, 0, 0:PAD]
        k_feat[head, 0, 0:PAD] = key
        v_feat[head, 0, 0:PAD] = value
        total = states[0, head] + outer(
            jnp.concatenate([key, old_key], axis=0), jnp.concatenate([value, -old_value], axis=0)
        )
        states[0, head] = jnp.zeros((HDIM, HDIM), f32)
        for chunk in range(1, chunks):
            own = states[chunk, head]
            states[chunk, head] = total
            total = total + own
        send1[head] = total.astype(bf16)

    def exchange(src, dst, send_sems, recv_sems, step):
        peer = mate(step)
        return pltpu.make_async_remote_copy(
            src_ref=src.at[lax.rem(member + step, heads)], dst_ref=dst.at[member],
            send_sem=send_sems.at[step], recv_sem=recv_sems.at[member],
            device_id={"ctx": peer}, device_id_type=MESH,
        )

    def arrival(src, dst, send_sems, recv_sems, step):
        source = lax.rem(member + heads - step, heads)
        return pltpu.make_async_remote_copy(
            src_ref=src.at[source], dst_ref=dst.at[source],
            send_sem=send_sems.at[step], recv_sem=recv_sems.at[source],
            device_id={"ctx": mate(step)}, device_id_type=MESH,
        )

    first = (send1, land1, send1_sems, recv1_sems)
    second = (send2, land2, send2_sems, recv2_sems)
    order = sorted(range(1, heads), key=lambda step: -min(step, heads - step))
    for step in order:
        exchange(*first, step).start()
    land1[member] = send1[member]

    g_load.wait()
    for chunk in range(chunks):
        load(0, chunk).wait()

    @pl.when(me > 0)
    def _():
        halo(0).wait_recv()

    @pl.loop(0, chunks)
    def _(chunk):
        rows = pl.ds(pl.multiple_of(chunk * CHUNK, CHUNK), CHUNK + PAD)
        row = lax.broadcasted_iota(jnp.int32, (CHUNK, CHUNK), 0)
        col = lax.broadcasted_iota(jnp.int32, (CHUNK, CHUNK), 1)
        for head in range(heads):
            wide[head] = q_raw[rows, lanes_of(head)].astype(f32)
            feat = (silu(conv(wide.at[head], taps(0, head, 0.5), CHUNK)) * HDIM ** (-0.5)).astype(bf16)
            q_feat[head, chunk] = feat
            scores = lax.dot_general(
                feat, k_feat[head, chunk], (((1,), (1,)), ((), ())), preferred_element_type=f32
            )
            scores = jnp.where(row >= col, scores, 0.0).astype(bf16)
            inner[head, chunk] = jnp.dot(scores, v_feat[head, chunk], preferred_element_type=f32)

    for step in order:
        arrival(*first, step).wait_recv()
    total = land1[0].astype(f32)
    for source in range(1, heads):
        total = total + land1[source].astype(f32)
    send3[...] = total.astype(bf16)

    def onward(other):
        return pltpu.make_async_remote_copy(
            src_ref=send3, dst_ref=land3.at[group], send_sem=send3_sems.at[other], recv_sem=recv3_sems.at[group],
            device_id={"ctx": other * heads + member}, device_id_type=MESH,
        )

    def upstream(other):
        return pltpu.make_async_remote_copy(
            src_ref=send3, dst_ref=land3.at[other], send_sem=send3_sems.at[other], recv_sem=recv3_sems.at[other],
            device_id={"ctx": lax.rem(me + heads, n)}, device_id_type=MESH,
        )

    for other in range(1, groups):
        @pl.when(group < other)
        def _():
            pl.semaphore_wait(ready_sems.at[other], 1)
            onward(other).start()
    for other in range(groups - 1):
        @pl.when(group > other)
        def _():
            upstream(other).wait_recv()

    total = land3[0].astype(f32)
    for other in range(1, groups - 1):
        total = total + land3[other].astype(f32)
    for source in range(heads):
        send2[source] = total.astype(bf16)
        total = total + land1[source].astype(f32)
    for step in order:
        exchange(*second, step).start()
    land2[member] = send2[member]
    for step in order:
        arrival(*second, step).wait_recv()

    def store(chunk):
        rows = pl.ds(pl.multiple_of(chunk * CHUNK, CHUNK), CHUNK)
        return pltpu.make_async_copy(out_buf.at[rows], out_hbm.at[rows], out_sems.at[chunk])

    @pl.loop(0, chunks)
    def _(chunk):
        rows = pl.ds(pl.multiple_of(chunk * CHUNK, CHUNK), CHUNK)
        ones = jnp.full((HDIM, HDIM), 1 / HDIM, bf16)
        for head in range(heads):
            prefix = (land2[head].astype(f32) + states[chunk, head]).astype(bf16)
            outputs = inner[head, chunk] + jnp.dot(q_feat[head, chunk], prefix, preferred_element_type=f32)
            mean = jnp.dot((outputs * outputs).astype(bf16), ones, preferred_element_type=f32)
            scaled = outputs * lax.rsqrt(mean + 1e-06) * g_ref[0:1, lanes_of(head)]
            out_buf[rows, lanes_of(head)] = scaled.astype(bf16)
        store(chunk).start()

    @pl.when(me < n - 1)
    def _():
        for kind in range(3):
            halo(kind).wait_send()

    for step in order:
        exchange(*first, step).wait_send()
        exchange(*second, step).wait_send()
    for other in range(1, groups):
        @pl.when(group < other)
        def _():
            onward(other).wait_send()
    for chunk in range(chunks):
        store(chunk).wait()


def body(queries, key_rows, value_rows, conv_weight, head_gain):
    tokens, width = queries.shape
    heads = width // HDIM
    n = lax.axis_size("ctx")
    groups = n // heads
    chunks = tokens // CHUNK
    bf16, f32 = jnp.bfloat16, jnp.float32
    dma = pltpu.SemaphoreType.DMA
    operands = (queries, key_rows, value_rows, conv_weight, head_gain.reshape(1, width))
    return pl.pallas_call(
        functools.partial(kernel, n, heads, tokens),
        out_shape=jax.ShapeDtypeStruct((tokens, width), bf16),
        in_specs=[pl.BlockSpec(memory_space=pltpu.HBM)] * 5,
        out_specs=pl.BlockSpec(memory_space=pl.ANY),
        scratch_shapes=[
            *[pltpu.VMEM((tokens + PAD, width), bf16)] * 3,
            *[pltpu.VMEM((TAIL, width), bf16)] * 2,
            pltpu.VMEM((3, CONV, width), f32),
            pltpu.VMEM((1, width), f32),
            *[pltpu.VMEM((heads, chunks, CHUNK, HDIM), bf16)] * 3,
            pltpu.VMEM((heads, chunks, CHUNK, HDIM), f32),
            pltpu.VMEM((chunks, heads, HDIM, HDIM), f32),
            *[pltpu.VMEM((heads, HDIM, HDIM), bf16)] * 4,
            pltpu.VMEM((HDIM, HDIM), bf16),
            pltpu.VMEM((groups - 1, HDIM, HDIM), bf16),
            pltpu.VMEM((tokens, width), bf16),
            pltpu.VMEM((2 * heads, CHUNK + PAD, HDIM), f32),
            dma((4, chunks)), dma((3,)), dma((3,)),
            dma((heads,)), dma((heads,)), dma((heads,)), dma((heads,)), dma((groups,)), dma((groups,)),
            pltpu.SemaphoreType.REGULAR((groups,)), dma((chunks,)),
        ],
        compiler_params=pltpu.CompilerParams(
            collective_id=0, has_side_effects=True, vmem_limit_bytes=48 * 1024 * 1024
        ),
        name="linear_attention",
    )(*[pltpu.with_memory_space_constraint(x, pltpu.HBM) for x in operands])


def solution(mesh):
    return jax.shard_map(
        body,
        mesh=mesh,
        in_specs=(
            P(("mp", "ctx"), None),
            P(("mp", "ctx"), None),
            P(("mp", "ctx"), None),
            P("mp", None, None),
            P("mp"),
        ),
        out_specs=P(("mp", "ctx"), None),
        check_vma=False,
    )
```

```python
import functools

import jax
import jax.numpy as jnp
from jax import lax
from jax.experimental import pallas as pl
from jax.experimental.pallas import tpu as pltpu
from jax.sharding import PartitionSpec as P

HDIM = 128
CONV = 4
PAD = 16
TAIL = 8
CHUNK = 256
HALO_AT = 1
MESH = pl.DeviceIdType.MESH


def conv(wide, weights, rows):
    terms = [weights[tap] * wide[pl.ds(PAD - CONV + 1 + tap, rows)] for tap in range(CONV)]
    return (terms[3] + terms[2]) + (terms[1] + terms[0])


def kernel(
    n, heads, tokens,
    q_hbm, k_hbm, v_hbm, w_hbm, g_hbm, out_ref,
    q_raw, k_raw, v_raw, halo_k, halo_v, w_ref, g_ref, q_feat, k_feat, v_feat,
    inner, states, send1, land1, send2, land2, send3, land3, wide,
    load_sems, halo_send, halo_recv, send1_sems, recv1_sems, send2_sems, recv2_sems, send3_sems, recv3_sems,
    ready_sems,
):
    me = lax.axis_index("ctx")
    groups = n // heads
    group, member = me // heads, lax.rem(me, heads)
    chunks = tokens // CHUNK
    bf16, f32 = jnp.bfloat16, jnp.float32

    def mate(step):
        return group * heads + lax.rem(member + step, heads)

    barrier = pltpu.get_barrier_semaphore()

    def greet(peer):
        pl.semaphore_signal(barrier, inc=1, device_id={"ctx": peer}, device_id_type=MESH)

    for step in range(1, heads):
        greet(mate(step))
    for other in range(1, groups):
        @pl.when(group < other)
        def _():
            greet(other * heads + member)

    @pl.when(jnp.logical_and(member == 0, group > 0))
    def _():
        greet(me - 1)

    w_load = pltpu.make_async_copy(w_hbm, w_ref, load_sems.at[3, 0])
    g_load = pltpu.make_async_copy(g_hbm, g_ref, load_sems.at[3, 1])

    def load(kind, chunk):
        rows = chunk * CHUNK
        return pltpu.make_async_copy(
            (q_hbm, k_hbm, v_hbm)[kind].at[pl.ds(rows, CHUNK)],
            (q_raw, k_raw, v_raw)[kind].at[pl.ds(PAD + rows, CHUNK)],
            load_sems.at[kind, chunk],
        )

    w_load.start()
    for chunk in range(chunks):
        load(1, chunk).start()
        load(2, chunk).start()
    g_load.start()
    for chunk in range(chunks):
        load(0, chunk).start()

    k_raw[0:PAD] = jnp.zeros((PAD, heads * HDIM), bf16)
    v_raw[0:PAD] = jnp.zeros((PAD, heads * HDIM), bf16)

    @pl.when(me == 0)
    def _():
        q_raw[0:PAD] = jnp.zeros((PAD, heads * HDIM), bf16)
        halo_k[...] = jnp.zeros((TAIL, heads * HDIM), bf16)
        halo_v[...] = jnp.zeros((TAIL, heads * HDIM), bf16)

    for other in range(groups - 1):
        @pl.when(group <= other)
        def _():
            land3[other] = jnp.zeros((HDIM, HDIM), bf16)

    def halo(kind):
        return pltpu.make_async_remote_copy(
            src_ref=(q_hbm, k_hbm, v_hbm)[kind].at[pl.ds(tokens - TAIL, TAIL)],
            dst_ref=(q_raw.at[pl.ds(PAD - TAIL, TAIL)], halo_k, halo_v)[kind],
            send_sem=halo_send.at[kind],
            recv_sem=halo_recv.at[kind],
            device_id={"ctx": lax.rem(me + 1, n)},
            device_id_type=MESH,
        )

    def lanes_of(head):
        return pl.ds(head * HDIM, HDIM)

    def taps(kind, head, factor=None):
        weights = [w_ref[kind, tap : tap + 1, lanes_of(head)] for tap in range(CONV)]
        return weights if factor is None else [weight * factor for weight in weights]

    def silu(half):
        return half + half * jnp.tanh(half)

    def outer(key, value):
        return lax.dot_general(key, value, (((0,), (0,)), ((), ())), preferred_element_type=f32)

    def meet():
        waits = heads - 1 + group + jnp.logical_and(member == heads - 1, group < groups - 1).astype(jnp.int32)
        pl.semaphore_wait(barrier, waits)

        @pl.when(me < n - 1)
        def _():
            for kind in (1, 2, 0):
                halo(kind).start()

        for other in range(groups - 1):
            @pl.when(group > other)
            def _():
                pl.semaphore_signal(
                    ready_sems.at[group], inc=1, device_id={"ctx": other * heads + member}, device_id_type=MESH
                )

    w_load.wait()

    @pl.loop(0, chunks)
    def _(chunk):
        @pl.when(chunk == HALO_AT)
        def _():
            meet()

        load(1, chunk).wait()
        load(2, chunk).wait()
        rows = pl.ds(pl.multiple_of(chunk * CHUNK, CHUNK), CHUNK + PAD)
        for head in range(heads):
            wide[2 * head] = k_raw[rows, lanes_of(head)].astype(f32)
            key = silu(conv(wide.at[2 * head], taps(1, head, 0.5), CHUNK)).astype(bf16)
            wide[2 * head + 1] = v_raw[rows, lanes_of(head)].astype(f32)
            value = conv(wide.at[2 * head + 1], taps(2, head), CHUNK).astype(bf16)
            k_feat[head, chunk] = key
            v_feat[head, chunk] = value
            states[chunk, head] = outer(key, value)

    @pl.when(me > 0)
    def _():
        halo(1).wait_recv()
        halo(2).wait_recv()

    for head in range(heads):
        new = []
        for kind, raw, tail in ((1, k_raw, halo_k), (2, v_raw, halo_v)):
            slot = wide.at[2 * head + kind - 1]
            slot[PAD - TAIL : PAD] = tail[:, lanes_of(head)].astype(f32)
            slot[PAD : 2 * PAD] = raw[PAD : 2 * PAD, lanes_of(head)].astype(f32)
            new.append(conv(slot, taps(kind, head, 0.5 if kind == 1 else None), PAD))
        key, value = silu(new[0]).astype(bf16), new[1].astype(bf16)
        old_key, old_value = k_feat[head, 0, 0:PAD], v_feat[head, 0, 0:PAD]
        k_feat[head, 0, 0:PAD] = key
        v_feat[head, 0, 0:PAD] = value
        total = states[0, head] + outer(
            jnp.concatenate([key, old_key], axis=0), jnp.concatenate([value, -old_value], axis=0)
        )
        states[0, head] = jnp.zeros((HDIM, HDIM), f32)
        for chunk in range(1, chunks):
            own = states[chunk, head]
            states[chunk, head] = total
            total = total + own
        send1[head] = total.astype(bf16)

    def exchange(src, dst, send_sems, recv_sems, step):
        peer = mate(step)
        return pltpu.make_async_remote_copy(
            src_ref=src.at[lax.rem(member + step, heads)], dst_ref=dst.at[member],
            send_sem=send_sems.at[step], recv_sem=recv_sems.at[member],
            device_id={"ctx": peer}, device_id_type=MESH,
        )

    def arrival(src, dst, send_sems, recv_sems, step):
        source = lax.rem(member + heads - step, heads)
        return pltpu.make_async_remote_copy(
            src_ref=src.at[source], dst_ref=dst.at[source],
            send_sem=send_sems.at[step], recv_sem=recv_sems.at[source],
            device_id={"ctx": mate(step)}, device_id_type=MESH,
        )

    first = (send1, land1, send1_sems, recv1_sems)
    second = (send2, land2, send2_sems, recv2_sems)
    order = sorted(range(1, heads), key=lambda step: min(step, heads - step))
    for step in order:
        exchange(*first, step).start()
    land1[member] = send1[member]

    g_load.wait()
    for chunk in range(chunks):
        load(0, chunk).wait()

    @pl.when(me > 0)
    def _():
        halo(0).wait_recv()

    @pl.loop(0, chunks)
    def _(chunk):
        rows = pl.ds(pl.multiple_of(chunk * CHUNK, CHUNK), CHUNK + PAD)
        row = lax.broadcasted_iota(jnp.int32, (CHUNK, CHUNK), 0)
        col = lax.broadcasted_iota(jnp.int32, (CHUNK, CHUNK), 1)
        for head in range(heads):
            wide[head] = q_raw[rows, lanes_of(head)].astype(f32)
            feat = (silu(conv(wide.at[head], taps(0, head, 0.5), CHUNK)) * HDIM ** (-0.5)).astype(bf16)
            q_feat[head, chunk] = feat
            scores = lax.dot_general(
                feat, k_feat[head, chunk], (((1,), (1,)), ((), ())), preferred_element_type=f32
            )
            scores = jnp.where(row >= col, scores, 0.0).astype(bf16)
            inner[head, chunk] = jnp.dot(scores, v_feat[head, chunk], preferred_element_type=f32)

    for step in order:
        arrival(*first, step).wait_recv()
    total = land1[0].astype(f32)
    for source in range(1, heads):
        total = total + land1[source].astype(f32)
    send3[...] = total.astype(bf16)

    def onward(other):
        return pltpu.make_async_remote_copy(
            src_ref=send3, dst_ref=land3.at[group], send_sem=send3_sems.at[other], recv_sem=recv3_sems.at[group],
            device_id={"ctx": other * heads + member}, device_id_type=MESH,
        )

    def upstream(other):
        return pltpu.make_async_remote_copy(
            src_ref=send3, dst_ref=land3.at[other], send_sem=send3_sems.at[other], recv_sem=recv3_sems.at[other],
            device_id={"ctx": lax.rem(me + heads, n)}, device_id_type=MESH,
        )

    for other in range(1, groups):
        @pl.when(group < other)
        def _():
            pl.semaphore_wait(ready_sems.at[other], 1)
            onward(other).start()
    for other in range(groups - 1):
        @pl.when(group > other)
        def _():
            upstream(other).wait_recv()

    total = land3[0].astype(f32)
    for other in range(1, groups - 1):
        total = total + land3[other].astype(f32)
    for source in range(heads):
        send2[source] = total.astype(bf16)
        total = total + land1[source].astype(f32)
    for step in order:
        exchange(*second, step).start()
    land2[member] = send2[member]
    ones = jnp.full((HDIM, HDIM), 1 / HDIM, bf16)

    def finish(head):
        lanes = pl.ds(pl.multiple_of(head * HDIM, HDIM), HDIM)
        gain = g_ref[0:1, lanes]
        prefix = land2[head].astype(f32)
        for chunk in range(chunks):
            outputs = inner[head, chunk] + jnp.dot(
                q_feat[head, chunk], (prefix + states[chunk, head]).astype(bf16), preferred_element_type=f32
            )
            mean = jnp.dot((outputs * outputs).astype(bf16), ones, preferred_element_type=f32)
            scaled = outputs * lax.rsqrt(mean + 1e-06) * gain
            out_ref[pl.ds(chunk * CHUNK, CHUNK), lanes] = scaled.astype(bf16)

    finish(member)
    for step in order:
        arrival(*second, step).wait_recv()
        finish(lax.rem(member + heads - step, heads))

    @pl.when(me < n - 1)
    def _():
        for kind in range(3):
            halo(kind).wait_send()

    for step in order:
        exchange(*first, step).wait_send()
        exchange(*second, step).wait_send()
    for other in range(1, groups):
        @pl.when(group < other)
        def _():
            onward(other).wait_send()


def body(queries, key_rows, value_rows, conv_weight, head_gain):
    tokens, width = queries.shape
    heads = width // HDIM
    n = lax.axis_size("ctx")
    groups = n // heads
    chunks = tokens // CHUNK
    bf16, f32 = jnp.bfloat16, jnp.float32
    dma = pltpu.SemaphoreType.DMA
    operands = (queries, key_rows, value_rows, conv_weight, head_gain.reshape(1, width))
    return pl.pallas_call(
        functools.partial(kernel, n, heads, tokens),
        out_shape=jax.ShapeDtypeStruct((tokens, width), bf16),
        in_specs=[pl.BlockSpec(memory_space=pltpu.HBM)] * 5,
        out_specs=pl.BlockSpec(memory_space=pltpu.VMEM),
        scratch_shapes=[
            *[pltpu.VMEM((tokens + PAD, width), bf16)] * 3,
            *[pltpu.VMEM((TAIL, width), bf16)] * 2,
            pltpu.VMEM((3, CONV, width), f32),
            pltpu.VMEM((1, width), f32),
            *[pltpu.VMEM((heads, chunks, CHUNK, HDIM), bf16)] * 3,
            pltpu.VMEM((heads, chunks, CHUNK, HDIM), f32),
            pltpu.VMEM((chunks, heads, HDIM, HDIM), f32),
            *[pltpu.VMEM((heads, HDIM, HDIM), bf16)] * 4,
            pltpu.VMEM((HDIM, HDIM), bf16),
            pltpu.VMEM((groups - 1, HDIM, HDIM), bf16),
            pltpu.VMEM((2 * heads, CHUNK + PAD, HDIM), f32),
            dma((4, chunks)), dma((3,)), dma((3,)),
            dma((heads,)), dma((heads,)), dma((heads,)), dma((heads,)), dma((groups,)), dma((groups,)),
            pltpu.SemaphoreType.REGULAR((groups,)),
        ],
        compiler_params=pltpu.CompilerParams(
            collective_id=0, has_side_effects=True, vmem_limit_bytes=48 * 1024 * 1024
        ),
        name="linear_attention",
    )(*[pltpu.with_memory_space_constraint(x, pltpu.HBM) for x in operands])


def solution(mesh):
    return jax.shard_map(
        body,
        mesh=mesh,
        in_specs=(
            P(("mp", "ctx"), None),
            P(("mp", "ctx"), None),
            P(("mp", "ctx"), None),
            P("mp", None, None),
            P("mp"),
        ),
        out_specs=P(("mp", "ctx"), None),
        check_vma=False,
    )
```

```python
import functools

import jax
import jax.numpy as jnp
from jax import lax
from jax.experimental import pallas as pl
from jax.experimental.pallas import tpu as pltpu
from jax.sharding import PartitionSpec as P

HDIM = 128
CONV = 4
PAD = 16
TAIL = 8
CHUNK = 256
HALO_AT = 1
MESH = pl.DeviceIdType.MESH


def conv(wide, weights, rows):
    terms = [weights[tap] * wide[pl.ds(PAD - CONV + 1 + tap, rows)] for tap in range(CONV)]
    return (terms[3] + terms[2]) + (terms[1] + terms[0])


def kernel(
    n, heads, tokens,
    q_hbm, k_hbm, v_hbm, w_hbm, g_hbm, out_ref,
    q_raw, k_raw, v_raw, halo_k, halo_v, w_ref, g_ref, q_feat, k_feat, v_feat,
    inner, states, whole0, whole1, squares0, squares1, send1, land1, send2, land2, send3, land3, wide,
    load_sems, halo_send, halo_recv, send1_sems, recv1_sems, send2_sems, recv2_sems, send3_sems, recv3_sems,
    ready_sems,
):
    me = lax.axis_index("ctx")
    groups = n // heads
    group, member = me // heads, lax.rem(me, heads)
    chunks = tokens // CHUNK
    bf16, f32 = jnp.bfloat16, jnp.float32
    whole, squares = (whole0, whole1), (squares0, squares1)

    def partner(mask):
        found, bit = member, 1
        while bit < heads:
            if mask & bit:
                found = found + bit * (1 - 2 * lax.rem(member // bit, 2))
            bit *= 2
        return found

    def mate(mask):
        return group * heads + partner(mask)

    barrier = pltpu.get_barrier_semaphore()

    def greet(peer):
        pl.semaphore_signal(barrier, inc=1, device_id={"ctx": peer}, device_id_type=MESH)

    for step in range(1, heads):
        greet(mate(step))
    for other in range(1, groups):
        @pl.when(group < other)
        def _():
            greet(other * heads + member)

    @pl.when(jnp.logical_and(member == 0, group > 0))
    def _():
        greet(me - 1)

    w_load = pltpu.make_async_copy(w_hbm, w_ref, load_sems.at[3, 0])
    g_load = pltpu.make_async_copy(g_hbm, g_ref, load_sems.at[3, 1])

    def load(kind, chunk):
        rows = chunk * CHUNK
        return pltpu.make_async_copy(
            (q_hbm, k_hbm, v_hbm)[kind].at[pl.ds(rows, CHUNK)],
            (q_raw, k_raw, v_raw)[kind].at[pl.ds(PAD + rows, CHUNK)],
            load_sems.at[kind, chunk],
        )

    w_load.start()
    for chunk in range(chunks):
        load(1, chunk).start()
        load(2, chunk).start()
    g_load.start()
    for chunk in range(chunks):
        load(0, chunk).start()

    k_raw[0:PAD] = jnp.zeros((PAD, heads * HDIM), bf16)
    v_raw[0:PAD] = jnp.zeros((PAD, heads * HDIM), bf16)

    @pl.when(me == 0)
    def _():
        q_raw[0:PAD] = jnp.zeros((PAD, heads * HDIM), bf16)
        halo_k[...] = jnp.zeros((TAIL, heads * HDIM), bf16)
        halo_v[...] = jnp.zeros((TAIL, heads * HDIM), bf16)

    for other in range(groups - 1):
        @pl.when(group <= other)
        def _():
            land3[other] = jnp.zeros((HDIM, HDIM), bf16)

    def halo(kind):
        return pltpu.make_async_remote_copy(
            src_ref=(q_hbm, k_hbm, v_hbm)[kind].at[pl.ds(tokens - TAIL, TAIL)],
            dst_ref=(q_raw.at[pl.ds(PAD - TAIL, TAIL)], halo_k, halo_v)[kind],
            send_sem=halo_send.at[kind],
            recv_sem=halo_recv.at[kind],
            device_id={"ctx": lax.rem(me + 1, n)},
            device_id_type=MESH,
        )

    def lanes_of(head):
        return pl.ds(head * HDIM, HDIM)

    def taps(kind, head, factor=None):
        weights = [w_ref[kind, tap : tap + 1, lanes_of(head)] for tap in range(CONV)]
        return weights if factor is None else [weight * factor for weight in weights]

    def silu(half):
        return half + half * jnp.tanh(half)

    def outer(key, value):
        return lax.dot_general(key, value, (((0,), (0,)), ((), ())), preferred_element_type=f32)

    def meet():
        waits = heads - 1 + group + jnp.logical_and(member == heads - 1, group < groups - 1).astype(jnp.int32)
        pl.semaphore_wait(barrier, waits)

        @pl.when(me < n - 1)
        def _():
            for kind in (1, 2, 0):
                halo(kind).start()

        for other in range(groups - 1):
            @pl.when(group > other)
            def _():
                pl.semaphore_signal(
                    ready_sems.at[group], inc=1, device_id={"ctx": other * heads + member}, device_id_type=MESH
                )

    w_load.wait()

    @pl.loop(0, chunks)
    def _(chunk):
        @pl.when(chunk == HALO_AT)
        def _():
            meet()

        load(1, chunk).wait()
        load(2, chunk).wait()
        rows = pl.ds(pl.multiple_of(chunk * CHUNK, CHUNK), CHUNK + PAD)
        for head in range(heads):
            wide[2 * head] = k_raw[rows, lanes_of(head)].astype(f32)
            key = silu(conv(wide.at[2 * head], taps(1, head, 0.5), CHUNK)).astype(bf16)
            wide[2 * head + 1] = v_raw[rows, lanes_of(head)].astype(f32)
            value = conv(wide.at[2 * head + 1], taps(2, head), CHUNK).astype(bf16)
            k_feat[head, chunk] = key
            v_feat[head, chunk] = value
            states[chunk, head] = outer(key, value)

    @pl.when(me > 0)
    def _():
        halo(1).wait_recv()
        halo(2).wait_recv()

    for head in range(heads):
        new = []
        for kind, raw, tail in ((1, k_raw, halo_k), (2, v_raw, halo_v)):
            slot = wide.at[2 * head + kind - 1]
            slot[PAD - TAIL : PAD] = tail[:, lanes_of(head)].astype(f32)
            slot[PAD : 2 * PAD] = raw[PAD : 2 * PAD, lanes_of(head)].astype(f32)
            new.append(conv(slot, taps(kind, head, 0.5 if kind == 1 else None), PAD))
        key, value = silu(new[0]).astype(bf16), new[1].astype(bf16)
        old_key, old_value = k_feat[head, 0, 0:PAD], v_feat[head, 0, 0:PAD]
        k_feat[head, 0, 0:PAD] = key
        v_feat[head, 0, 0:PAD] = value
        total = states[0, head] + outer(
            jnp.concatenate([key, old_key], axis=0), jnp.concatenate([value, -old_value], axis=0)
        )
        states[0, head] = jnp.zeros((HDIM, HDIM), f32)
        for chunk in range(1, chunks):
            own = states[chunk, head]
            states[chunk, head] = total
            total = total + own
        send1[head] = total.astype(bf16)

    def exchange(src, dst, send_sems, recv_sems, step):
        peer = mate(step)
        return pltpu.make_async_remote_copy(
            src_ref=src.at[partner(step)], dst_ref=dst.at[member],
            send_sem=send_sems.at[step], recv_sem=recv_sems.at[member],
            device_id={"ctx": peer}, device_id_type=MESH,
        )

    def arrival(src, dst, send_sems, recv_sems, step):
        source = partner(step)
        return pltpu.make_async_remote_copy(
            src_ref=src.at[source], dst_ref=dst.at[source],
            send_sem=send_sems.at[step], recv_sem=recv_sems.at[source],
            device_id={"ctx": mate(step)}, device_id_type=MESH,
        )

    first = (send1, land1, send1_sems, recv1_sems)
    second = (send2, land2, send2_sems, recv2_sems)
    order = [1, 3, 4, 2, 5, 7, 6]
    for step in order:
        exchange(*first, step).start()
    land1[member] = send1[member]

    g_load.wait()
    for chunk in range(chunks):
        load(0, chunk).wait()

    @pl.when(me > 0)
    def _():
        halo(0).wait_recv()

    @pl.loop(0, chunks)
    def _(chunk):
        rows = pl.ds(pl.multiple_of(chunk * CHUNK, CHUNK), CHUNK + PAD)
        row = lax.broadcasted_iota(jnp.int32, (CHUNK, CHUNK), 0)
        col = lax.broadcasted_iota(jnp.int32, (CHUNK, CHUNK), 1)
        for head in range(heads):
            wide[head] = q_raw[rows, lanes_of(head)].astype(f32)
            feat = (silu(conv(wide.at[head], taps(0, head, 0.5), CHUNK)) * HDIM ** (-0.5)).astype(bf16)
            q_feat[head, chunk] = feat
            scores = lax.dot_general(
                feat, k_feat[head, chunk], (((1,), (1,)), ((), ())), preferred_element_type=f32
            )
            scores = jnp.where(row >= col, scores, 0.0).astype(bf16)
            inner[head, chunk] = jnp.dot(scores, v_feat[head, chunk], preferred_element_type=f32)

    for step in order:
        arrival(*first, step).wait_recv()
    total = land1[0].astype(f32)
    for source in range(1, heads):
        total = total + land1[source].astype(f32)
    send3[...] = total.astype(bf16)

    def onward(other):
        return pltpu.make_async_remote_copy(
            src_ref=send3, dst_ref=land3.at[group], send_sem=send3_sems.at[other], recv_sem=recv3_sems.at[group],
            device_id={"ctx": other * heads + member}, device_id_type=MESH,
        )

    def upstream(other):
        return pltpu.make_async_remote_copy(
            src_ref=send3, dst_ref=land3.at[other], send_sem=send3_sems.at[other], recv_sem=recv3_sems.at[other],
            device_id={"ctx": lax.rem(me + heads, n)}, device_id_type=MESH,
        )

    for other in range(1, groups):
        @pl.when(group < other)
        def _():
            pl.semaphore_wait(ready_sems.at[other], 1)
            onward(other).start()
    for other in range(groups - 1):
        @pl.when(group > other)
        def _():
            upstream(other).wait_recv()

    total = land3[0].astype(f32)
    for other in range(1, groups - 1):
        total = total + land3[other].astype(f32)
    for source in range(heads):
        send2[source] = total.astype(bf16)
        total = total + land1[source].astype(f32)
    for step in order:
        exchange(*second, step).start()
    land2[member] = send2[member]
    ones = jnp.full((HDIM, HDIM), 1 / HDIM, bf16)

    def add_prefix(head, place):
        prefix = land2[head].astype(f32)
        for chunk in range(chunks):
            outputs = inner[head, chunk] + jnp.dot(
                q_feat[head, chunk], (prefix + states[chunk, head]).astype(bf16), preferred_element_type=f32
            )
            whole[place % 2][chunk] = outputs
            squares[place % 2][chunk] = (outputs * outputs).astype(bf16)

    def norm(head, place):
        lanes = pl.ds(pl.multiple_of(head * HDIM, HDIM), HDIM)
        gain = g_ref[0:1, lanes]
        for chunk in range(chunks):
            mean = jnp.dot(squares[place % 2][chunk], ones, preferred_element_type=f32)
            scaled = whole[place % 2][chunk] * lax.rsqrt(mean + 1e-06) * gain
            out_ref[pl.ds(chunk * CHUNK, CHUNK), lanes] = scaled.astype(bf16)

    add_prefix(member, 0)
    last = member
    for place, step in enumerate(order):
        arrival(*second, step).wait_recv()
        add_prefix(partner(step), place + 1)
        norm(last, place)
        last = partner(step)
    norm(last, len(order))

    @pl.when(me < n - 1)
    def _():
        for kind in range(3):
            halo(kind).wait_send()

    for step in order:
        exchange(*first, step).wait_send()
        exchange(*second, step).wait_send()
    for other in range(1, groups):
        @pl.when(group < other)
        def _():
            onward(other).wait_send()


def body(queries, key_rows, value_rows, conv_weight, head_gain):
    tokens, width = queries.shape
    heads = width // HDIM
    n = lax.axis_size("ctx")
    groups = n // heads
    chunks = tokens // CHUNK
    bf16, f32 = jnp.bfloat16, jnp.float32
    dma = pltpu.SemaphoreType.DMA
    operands = (queries, key_rows, value_rows, conv_weight, head_gain.reshape(1, width))
    return pl.pallas_call(
        functools.partial(kernel, n, heads, tokens),
        out_shape=jax.ShapeDtypeStruct((tokens, width), bf16),
        in_specs=[pl.BlockSpec(memory_space=pltpu.HBM)] * 5,
        out_specs=pl.BlockSpec(memory_space=pltpu.VMEM),
        scratch_shapes=[
            *[pltpu.VMEM((tokens + PAD, width), bf16)] * 3,
            *[pltpu.VMEM((TAIL, width), bf16)] * 2,
            pltpu.VMEM((3, CONV, width), f32),
            pltpu.VMEM((1, width), f32),
            *[pltpu.VMEM((heads, chunks, CHUNK, HDIM), bf16)] * 3,
            pltpu.VMEM((heads, chunks, CHUNK, HDIM), f32),
            pltpu.VMEM((chunks, heads, HDIM, HDIM), f32),
            *[pltpu.VMEM((chunks, CHUNK, HDIM), f32)] * 2,
            *[pltpu.VMEM((chunks, CHUNK, HDIM), bf16)] * 2,
            *[pltpu.VMEM((heads, HDIM, HDIM), bf16)] * 4,
            pltpu.VMEM((HDIM, HDIM), bf16),
            pltpu.VMEM((groups - 1, HDIM, HDIM), bf16),
            pltpu.VMEM((2 * heads, CHUNK + PAD, HDIM), f32),
            dma((4, chunks)), dma((3,)), dma((3,)),
            dma((heads,)), dma((heads,)), dma((heads,)), dma((heads,)), dma((groups,)), dma((groups,)),
            pltpu.SemaphoreType.REGULAR((groups,)),
        ],
        compiler_params=pltpu.CompilerParams(
            collective_id=0, has_side_effects=True, vmem_limit_bytes=48 * 1024 * 1024
        ),
        name="linear_attention",
    )(*[pltpu.with_memory_space_constraint(x, pltpu.HBM) for x in operands])


def solution(mesh):
    return jax.shard_map(
        body,
        mesh=mesh,
        in_specs=(
            P(("mp", "ctx"), None),
            P(("mp", "ctx"), None),
            P(("mp", "ctx"), None),
            P("mp", None, None),
            P("mp"),
        ),
        out_specs=P(("mp", "ctx"), None),
        check_vma=False,
    )
```

```python
import functools

import jax
import jax.numpy as jnp
from jax import lax
from jax.experimental import pallas as pl
from jax.experimental.pallas import tpu as pltpu
from jax.sharding import PartitionSpec as P

HDIM = 128
CONV = 4
PAD = 16
TAIL = 8
CHUNK = 256
HALO_AT = 1
MESH = pl.DeviceIdType.MESH


def conv(wide, weights, rows):
    terms = [weights[tap] * wide[pl.ds(PAD - CONV + 1 + tap, rows)] for tap in range(CONV)]
    return (terms[3] + terms[2]) + (terms[1] + terms[0])


def kernel(
    n, heads, tokens,
    q_hbm, k_hbm, v_hbm, w_hbm, g_hbm, out_ref,
    q_raw, k_raw, v_raw, halo_k, halo_v, w_ref, g_ref, q_feat, k_feat, v_feat,
    inner, states, whole0, whole1, squares0, squares1, send1, land1, send2, land2, send3, land3, wide,
    load_sems, halo_send, halo_recv, send1_sems, recv1_sems, send2_sems, recv2_sems, send3_sems, recv3_sems,
    ready_sems,
):
    me = lax.axis_index("ctx")
    groups = n // heads
    group, member = me // heads, lax.rem(me, heads)
    chunks = tokens // CHUNK
    bf16, f32 = jnp.bfloat16, jnp.float32
    whole, squares = (whole0, whole1), (squares0, squares1)

    def partner(mask):
        found, bit = member, 1
        while bit < heads:
            if mask & bit:
                found = found + bit * (1 - 2 * lax.rem(member // bit, 2))
            bit *= 2
        return found

    def mate(mask):
        return group * heads + partner(mask)

    w_load = pltpu.make_async_copy(w_hbm, w_ref, load_sems.at[3, 0])
    g_load = pltpu.make_async_copy(g_hbm, g_ref, load_sems.at[3, 1])

    def load(kind, chunk):
        rows = chunk * CHUNK
        return pltpu.make_async_copy(
            (q_hbm, k_hbm, v_hbm)[kind].at[pl.ds(rows, CHUNK)],
            (q_raw, k_raw, v_raw)[kind].at[pl.ds(PAD + rows, CHUNK)],
            load_sems.at[kind, chunk],
        )

    w_load.start()
    load(1, 0).start()
    load(2, 0).start()

    barrier = pltpu.get_barrier_semaphore()

    def greet(peer):
        pl.semaphore_signal(barrier, inc=1, device_id={"ctx": peer}, device_id_type=MESH)

    for step in range(1, heads):
        greet(mate(step))
    for other in range(1, groups):
        @pl.when(group < other)
        def _():
            greet(other * heads + member)

    @pl.when(jnp.logical_and(member == 0, group > 0))
    def _():
        greet(me - 1)

    for chunk in range(1, chunks):
        load(1, chunk).start()
        load(2, chunk).start()
    g_load.start()
    for chunk in range(chunks):
        load(0, chunk).start()

    k_raw[0:PAD] = jnp.zeros((PAD, heads * HDIM), bf16)
    v_raw[0:PAD] = jnp.zeros((PAD, heads * HDIM), bf16)

    @pl.when(me == 0)
    def _():
        q_raw[0:PAD] = jnp.zeros((PAD, heads * HDIM), bf16)
        halo_k[...] = jnp.zeros((TAIL, heads * HDIM), bf16)
        halo_v[...] = jnp.zeros((TAIL, heads * HDIM), bf16)

    for other in range(groups - 1):
        @pl.when(group <= other)
        def _():
            land3[other] = jnp.zeros((HDIM, HDIM), bf16)

    def halo(kind):
        return pltpu.make_async_remote_copy(
            src_ref=(q_hbm, k_hbm, v_hbm)[kind].at[pl.ds(tokens - TAIL, TAIL)],
            dst_ref=(q_raw.at[pl.ds(PAD - TAIL, TAIL)], halo_k, halo_v)[kind],
            send_sem=halo_send.at[kind],
            recv_sem=halo_recv.at[kind],
            device_id={"ctx": lax.rem(me + 1, n)},
            device_id_type=MESH,
        )

    def lanes_of(head):
        return pl.ds(head * HDIM, HDIM)

    def taps(kind, head, factor=None):
        weights = [w_ref[kind, tap : tap + 1, lanes_of(head)] for tap in range(CONV)]
        return weights if factor is None else [weight * factor for weight in weights]

    def silu(half):
        return half + half * jnp.tanh(half)

    def outer(key, value):
        return lax.dot_general(key, value, (((0,), (0,)), ((), ())), preferred_element_type=f32)

    def meet():
        waits = heads - 1 + group + jnp.logical_and(member == heads - 1, group < groups - 1).astype(jnp.int32)
        pl.semaphore_wait(barrier, waits)

        @pl.when(me < n - 1)
        def _():
            for kind in (1, 2, 0):
                halo(kind).start()

        for other in range(groups - 1):
            @pl.when(group > other)
            def _():
                pl.semaphore_signal(
                    ready_sems.at[group], inc=1, device_id={"ctx": other * heads + member}, device_id_type=MESH
                )

    w_load.wait()

    @pl.loop(0, chunks)
    def _(chunk):
        @pl.when(chunk == HALO_AT)
        def _():
            meet()

        load(1, chunk).wait()
        load(2, chunk).wait()
        rows = pl.ds(pl.multiple_of(chunk * CHUNK, CHUNK), CHUNK + PAD)
        for head in range(heads):
            wide[2 * head] = k_raw[rows, lanes_of(head)].astype(f32)
            key = silu(conv(wide.at[2 * head], taps(1, head, 0.5), CHUNK)).astype(bf16)
            wide[2 * head + 1] = v_raw[rows, lanes_of(head)].astype(f32)
            value = conv(wide.at[2 * head + 1], taps(2, head), CHUNK).astype(bf16)
            k_feat[head, chunk] = key
            v_feat[head, chunk] = value
            states[chunk, head] = outer(key, value)

    @pl.when(me > 0)
    def _():
        halo(1).wait_recv()
        halo(2).wait_recv()

    for head in range(heads):
        new = []
        for kind, raw, tail in ((1, k_raw, halo_k), (2, v_raw, halo_v)):
            slot = wide.at[2 * head + kind - 1]
            slot[PAD - TAIL : PAD] = tail[:, lanes_of(head)].astype(f32)
            slot[PAD : 2 * PAD] = raw[PAD : 2 * PAD, lanes_of(head)].astype(f32)
            new.append(conv(slot, taps(kind, head, 0.5 if kind == 1 else None), PAD))
        key, value = silu(new[0]).astype(bf16), new[1].astype(bf16)
        old_key, old_value = k_feat[head, 0, 0:PAD], v_feat[head, 0, 0:PAD]
        k_feat[head, 0, 0:PAD] = key
        v_feat[head, 0, 0:PAD] = value
        total = states[0, head] + outer(
            jnp.concatenate([key, old_key], axis=0), jnp.concatenate([value, -old_value], axis=0)
        )
        states[0, head] = jnp.zeros((HDIM, HDIM), f32)
        for chunk in range(1, chunks):
            own = states[chunk, head]
            states[chunk, head] = total
            total = total + own
        send1[head] = total.astype(bf16)

    def exchange(src, dst, send_sems, recv_sems, step):
        peer = mate(step)
        return pltpu.make_async_remote_copy(
            src_ref=src.at[partner(step)], dst_ref=dst.at[member],
            send_sem=send_sems.at[step], recv_sem=recv_sems.at[member],
            device_id={"ctx": peer}, device_id_type=MESH,
        )

    def arrival(src, dst, send_sems, recv_sems, step):
        source = partner(step)
        return pltpu.make_async_remote_copy(
            src_ref=src.at[source], dst_ref=dst.at[source],
            send_sem=send_sems.at[step], recv_sem=recv_sems.at[source],
            device_id={"ctx": mate(step)}, device_id_type=MESH,
        )

    first = (send1, land1, send1_sems, recv1_sems)
    second = (send2, land2, send2_sems, recv2_sems)
    order = [1, 3, 4, 2, 5, 7, 6]
    for step in order:
        exchange(*first, step).start()
    land1[member] = send1[member]

    g_load.wait()
    for chunk in range(chunks):
        load(0, chunk).wait()

    @pl.when(me > 0)
    def _():
        halo(0).wait_recv()

    @pl.loop(0, chunks)
    def _(chunk):
        rows = pl.ds(pl.multiple_of(chunk * CHUNK, CHUNK), CHUNK + PAD)
        row = lax.broadcasted_iota(jnp.int32, (CHUNK, CHUNK), 0)
        col = lax.broadcasted_iota(jnp.int32, (CHUNK, CHUNK), 1)
        for head in range(heads):
            wide[head] = q_raw[rows, lanes_of(head)].astype(f32)
            feat = (silu(conv(wide.at[head], taps(0, head, 0.5), CHUNK)) * HDIM ** (-0.5)).astype(bf16)
            q_feat[head, chunk] = feat
            scores = lax.dot_general(
                feat, k_feat[head, chunk], (((1,), (1,)), ((), ())), preferred_element_type=f32
            )
            scores = jnp.where(row >= col, scores, 0.0).astype(bf16)
            inner[head, chunk] = jnp.dot(scores, v_feat[head, chunk], preferred_element_type=f32)

    for step in order:
        arrival(*first, step).wait_recv()
    total = land1[0].astype(f32)
    for source in range(1, heads):
        total = total + land1[source].astype(f32)
    send3[...] = total.astype(bf16)

    def onward(other):
        return pltpu.make_async_remote_copy(
            src_ref=send3, dst_ref=land3.at[group], send_sem=send3_sems.at[other], recv_sem=recv3_sems.at[group],
            device_id={"ctx": other * heads + member}, device_id_type=MESH,
        )

    def upstream(other):
        return pltpu.make_async_remote_copy(
            src_ref=send3, dst_ref=land3.at[other], send_sem=send3_sems.at[other], recv_sem=recv3_sems.at[other],
            device_id={"ctx": lax.rem(me + heads, n)}, device_id_type=MESH,
        )

    for other in range(1, groups):
        @pl.when(group < other)
        def _():
            pl.semaphore_wait(ready_sems.at[other], 1)
            onward(other).start()
    for other in range(groups - 1):
        @pl.when(group > other)
        def _():
            upstream(other).wait_recv()

    total = land3[0].astype(f32)
    for other in range(1, groups - 1):
        total = total + land3[other].astype(f32)
    for source in range(heads):
        send2[source] = total.astype(bf16)
        total = total + land1[source].astype(f32)
    for step in order:
        exchange(*second, step).start()
    land2[member] = send2[member]
    ones = jnp.full((HDIM, HDIM), 1 / HDIM, bf16)

    def add_prefix(head, place):
        prefix = land2[head].astype(f32)
        for chunk in range(chunks):
            outputs = inner[head, chunk] + jnp.dot(
                q_feat[head, chunk], (prefix + states[chunk, head]).astype(bf16), preferred_element_type=f32
            )
            whole[place % 2][chunk] = outputs
            squares[place % 2][chunk] = (outputs * outputs).astype(bf16)

    def norm(head, place):
        lanes = pl.ds(pl.multiple_of(head * HDIM, HDIM), HDIM)
        gain = g_ref[0:1, lanes]
        for chunk in range(chunks):
            mean = jnp.dot(squares[place % 2][chunk], ones, preferred_element_type=f32)
            scaled = whole[place % 2][chunk] * lax.rsqrt(mean + 1e-06) * gain
            out_ref[pl.ds(chunk * CHUNK, CHUNK), lanes] = scaled.astype(bf16)

    add_prefix(member, 0)
    last = member
    for place, step in enumerate(order):
        arrival(*second, step).wait_recv()
        add_prefix(partner(step), place + 1)
        norm(last, place)
        last = partner(step)
    norm(last, len(order))

    @pl.when(me < n - 1)
    def _():
        for kind in range(3):
            halo(kind).wait_send()

    for step in order:
        exchange(*first, step).wait_send()
        exchange(*second, step).wait_send()
    for other in range(1, groups):
        @pl.when(group < other)
        def _():
            onward(other).wait_send()


def body(queries, key_rows, value_rows, conv_weight, head_gain):
    tokens, width = queries.shape
    heads = width // HDIM
    n = lax.axis_size("ctx")
    groups = n // heads
    chunks = tokens // CHUNK
    bf16, f32 = jnp.bfloat16, jnp.float32
    dma = pltpu.SemaphoreType.DMA
    operands = (queries, key_rows, value_rows, conv_weight, head_gain.reshape(1, width))
    return pl.pallas_call(
        functools.partial(kernel, n, heads, tokens),
        out_shape=jax.ShapeDtypeStruct((tokens, width), bf16),
        in_specs=[pl.BlockSpec(memory_space=pltpu.HBM)] * 5,
        out_specs=pl.BlockSpec(memory_space=pltpu.VMEM),
        scratch_shapes=[
            *[pltpu.VMEM((tokens + PAD, width), bf16)] * 3,
            *[pltpu.VMEM((TAIL, width), bf16)] * 2,
            pltpu.VMEM((3, CONV, width), f32),
            pltpu.VMEM((1, width), f32),
            *[pltpu.VMEM((heads, chunks, CHUNK, HDIM), bf16)] * 3,
            pltpu.VMEM((heads, chunks, CHUNK, HDIM), f32),
            pltpu.VMEM((chunks, heads, HDIM, HDIM), f32),
            *[pltpu.VMEM((chunks, CHUNK, HDIM), f32)] * 2,
            *[pltpu.VMEM((chunks, CHUNK, HDIM), bf16)] * 2,
            *[pltpu.VMEM((heads, HDIM, HDIM), bf16)] * 4,
            pltpu.VMEM((HDIM, HDIM), bf16),
            pltpu.VMEM((groups - 1, HDIM, HDIM), bf16),
            pltpu.VMEM((2 * heads, CHUNK + PAD, HDIM), f32),
            dma((4, chunks)), dma((3,)), dma((3,)),
            dma((heads,)), dma((heads,)), dma((heads,)), dma((heads,)), dma((groups,)), dma((groups,)),
            pltpu.SemaphoreType.REGULAR((groups,)),
        ],
        compiler_params=pltpu.CompilerParams(
            collective_id=0, has_side_effects=True, vmem_limit_bytes=48 * 1024 * 1024
        ),
        name="linear_attention",
    )(*[pltpu.with_memory_space_constraint(x, pltpu.HBM) for x in operands])


def solution(mesh):
    return jax.shard_map(
        body,
        mesh=mesh,
        in_specs=(
            P(("mp", "ctx"), None),
            P(("mp", "ctx"), None),
            P(("mp", "ctx"), None),
            P("mp", None, None),
            P("mp"),
        ),
        out_specs=P(("mp", "ctx"), None),
        check_vma=False,
    )
```

```python
import functools

import jax
import jax.numpy as jnp
from jax import lax
from jax.experimental import pallas as pl
from jax.experimental.pallas import tpu as pltpu
from jax.sharding import PartitionSpec as P

HDIM = 128
CONV = 4
PAD = 16
TAIL = 8
CHUNK = 256
HALO_AT = 1
MESH = pl.DeviceIdType.MESH


def conv(wide, weights, rows):
    terms = [weights[tap] * wide[pl.ds(PAD - CONV + 1 + tap, rows)] for tap in range(CONV)]
    return (terms[3] + terms[2]) + (terms[1] + terms[0])


def kernel(
    n, heads, tokens,
    q_hbm, k_hbm, v_hbm, w_hbm, g_hbm, out_ref,
    q_raw, k_raw, v_raw, halo_k, halo_v, w_ref, g_ref, q_feat, k_feat, v_feat,
    inner, states, whole0, whole1, squares0, squares1, send1, land1, send2, land2, send3, land3, wide,
    load_sems, halo_send, halo_recv, send1_sems, recv1_sems, send2_sems, recv2_sems, send3_sems, recv3_sems,
    ready_sems,
):
    me = lax.axis_index("ctx")
    groups = n // heads
    group, member = me // heads, lax.rem(me, heads)
    chunks = tokens // CHUNK
    bf16, f32 = jnp.bfloat16, jnp.float32
    whole, squares = (whole0, whole1), (squares0, squares1)

    def partner(mask):
        found, bit = member, 1
        while bit < heads:
            if mask & bit:
                found = found + bit * (1 - 2 * lax.rem(member // bit, 2))
            bit *= 2
        return found

    def mate(mask):
        return group * heads + partner(mask)

    barrier = pltpu.get_barrier_semaphore()

    def greet(peer):
        pl.semaphore_signal(barrier, inc=1, device_id={"ctx": peer}, device_id_type=MESH)

    for step in range(1, heads):
        greet(mate(step))
    for other in range(1, groups):
        @pl.when(group < other)
        def _():
            greet(other * heads + member)

    @pl.when(jnp.logical_and(member == 0, group > 0))
    def _():
        greet(me - 1)

    w_load = pltpu.make_async_copy(w_hbm, w_ref, load_sems.at[3, 0])
    g_load = pltpu.make_async_copy(g_hbm, g_ref, load_sems.at[3, 1])

    def load(kind, chunk):
        rows = chunk * CHUNK
        return pltpu.make_async_copy(
            (q_hbm, k_hbm, v_hbm)[kind].at[pl.ds(rows, CHUNK)],
            (q_raw, k_raw, v_raw)[kind].at[pl.ds(PAD + rows, CHUNK)],
            load_sems.at[kind, chunk],
        )

    w_load.start()
    for chunk in range(chunks):
        load(1, chunk).start()
        load(2, chunk).start()
    g_load.start()
    for chunk in range(chunks):
        load(0, chunk).start()

    k_raw[0:PAD] = jnp.zeros((PAD, heads * HDIM), bf16)
    v_raw[0:PAD] = jnp.zeros((PAD, heads * HDIM), bf16)

    @pl.when(me == 0)
    def _():
        q_raw[0:PAD] = jnp.zeros((PAD, heads * HDIM), bf16)
        halo_k[...] = jnp.zeros((TAIL, heads * HDIM), bf16)
        halo_v[...] = jnp.zeros((TAIL, heads * HDIM), bf16)

    for other in range(groups - 1):
        @pl.when(group <= other)
        def _():
            land3[other] = jnp.zeros((HDIM, HDIM), bf16)

    def halo(kind):
        return pltpu.make_async_remote_copy(
            src_ref=(q_hbm, k_hbm, v_hbm)[kind].at[pl.ds(tokens - TAIL, TAIL)],
            dst_ref=(q_raw.at[pl.ds(PAD - TAIL, TAIL)], halo_k, halo_v)[kind],
            send_sem=halo_send.at[kind],
            recv_sem=halo_recv.at[kind],
            device_id={"ctx": lax.rem(me + 1, n)},
            device_id_type=MESH,
        )

    def lanes_of(head):
        return pl.ds(head * HDIM, HDIM)

    def taps(kind, head, factor=None):
        weights = [w_ref[kind, tap : tap + 1, lanes_of(head)] for tap in range(CONV)]
        return weights if factor is None else [weight * factor for weight in weights]

    def silu(half):
        return half + half * jnp.tanh(half)

    def outer(key, value):
        return lax.dot_general(key, value, (((0,), (0,)), ((), ())), preferred_element_type=f32)

    def meet():
        waits = heads - 1 + group + jnp.logical_and(member == heads - 1, group < groups - 1).astype(jnp.int32)
        pl.semaphore_wait(barrier, waits)

        @pl.when(me < n - 1)
        def _():
            for kind in (1, 2, 0):
                halo(kind).start()

        for other in range(groups - 1):
            @pl.when(group > other)
            def _():
                pl.semaphore_signal(
                    ready_sems.at[group], inc=1, device_id={"ctx": other * heads + member}, device_id_type=MESH
                )

    w_load.wait()

    @pl.loop(0, chunks)
    def _(chunk):
        @pl.when(chunk == HALO_AT)
        def _():
            meet()

        load(1, chunk).wait()
        load(2, chunk).wait()
        rows = pl.ds(pl.multiple_of(chunk * CHUNK, CHUNK), CHUNK + PAD)
        for head in range(heads):
            wide[2 * head] = k_raw[rows, lanes_of(head)].astype(f32)
            key = silu(conv(wide.at[2 * head], taps(1, head, 0.5), CHUNK)).astype(bf16)
            wide[2 * head + 1] = v_raw[rows, lanes_of(head)].astype(f32)
            value = conv(wide.at[2 * head + 1], taps(2, head), CHUNK).astype(bf16)
            k_feat[head, chunk] = key
            v_feat[head, chunk] = value
            states[chunk, head] = outer(key, value)

    @pl.when(me > 0)
    def _():
        halo(1).wait_recv()
        halo(2).wait_recv()

    for head in range(heads):
        new = []
        for kind, raw, tail in ((1, k_raw, halo_k), (2, v_raw, halo_v)):
            slot = wide.at[2 * head + kind - 1]
            slot[PAD - TAIL : PAD] = tail[:, lanes_of(head)].astype(f32)
            slot[PAD : 2 * PAD] = raw[PAD : 2 * PAD, lanes_of(head)].astype(f32)
            new.append(conv(slot, taps(kind, head, 0.5 if kind == 1 else None), PAD))
        key, value = silu(new[0]).astype(bf16), new[1].astype(bf16)
        old_key, old_value = k_feat[head, 0, 0:PAD], v_feat[head, 0, 0:PAD]
        k_feat[head, 0, 0:PAD] = key
        v_feat[head, 0, 0:PAD] = value
        total = states[0, head] + outer(
            jnp.concatenate([key, old_key], axis=0), jnp.concatenate([value, -old_value], axis=0)
        )
        states[0, head] = jnp.zeros((HDIM, HDIM), f32)
        for chunk in range(1, chunks):
            own = states[chunk, head]
            states[chunk, head] = total
            total = total + own
        send1[head] = total.astype(bf16)

    def exchange(src, dst, send_sems, recv_sems, step):
        peer = mate(step)
        return pltpu.make_async_remote_copy(
            src_ref=src.at[partner(step)], dst_ref=dst.at[member],
            send_sem=send_sems.at[step], recv_sem=recv_sems.at[member],
            device_id={"ctx": peer}, device_id_type=MESH,
        )

    def arrival(src, dst, send_sems, recv_sems, step):
        source = partner(step)
        return pltpu.make_async_remote_copy(
            src_ref=src.at[source], dst_ref=dst.at[source],
            send_sem=send_sems.at[step], recv_sem=recv_sems.at[source],
            device_id={"ctx": mate(step)}, device_id_type=MESH,
        )

    first = (send1, land1, send1_sems, recv1_sems)
    second = (send2, land2, send2_sems, recv2_sems)
    order = [1, 3, 4, 2, 5, 7, 6]
    for step in order:
        exchange(*first, step).start()
    land1[member] = send1[member]

    g_load.wait()
    for chunk in range(chunks):
        load(0, chunk).wait()

    @pl.when(me > 0)
    def _():
        halo(0).wait_recv()

    @pl.loop(0, chunks)
    def _(chunk):
        rows = pl.ds(pl.multiple_of(chunk * CHUNK, CHUNK), CHUNK + PAD)
        row = lax.broadcasted_iota(jnp.int32, (CHUNK, CHUNK), 0)
        col = lax.broadcasted_iota(jnp.int32, (CHUNK, CHUNK), 1)
        for head in range(heads):
            wide[head] = q_raw[rows, lanes_of(head)].astype(f32)
            feat = (silu(conv(wide.at[head], taps(0, head, 0.5), CHUNK)) * HDIM ** (-0.5)).astype(bf16)
            q_feat[head, chunk] = feat
            scores = lax.dot_general(
                feat, k_feat[head, chunk], (((1,), (1,)), ((), ())), preferred_element_type=f32
            )
            scores = jnp.where(row >= col, scores, 0.0).astype(bf16)
            inner[head, chunk] = jnp.dot(scores, v_feat[head, chunk], preferred_element_type=f32)

    for step in order:
        arrival(*first, step).wait_recv()
    total = land1[0].astype(f32)
    for source in range(1, heads):
        total = total + land1[source].astype(f32)
    send3[...] = total.astype(bf16)

    def onward(other):
        return pltpu.make_async_remote_copy(
            src_ref=send3, dst_ref=land3.at[group], send_sem=send3_sems.at[other], recv_sem=recv3_sems.at[group],
            device_id={"ctx": other * heads + member}, device_id_type=MESH,
        )

    def upstream(other):
        return pltpu.make_async_remote_copy(
            src_ref=send3, dst_ref=land3.at[other], send_sem=send3_sems.at[other], recv_sem=recv3_sems.at[other],
            device_id={"ctx": lax.rem(me + heads, n)}, device_id_type=MESH,
        )

    for other in range(1, groups):
        @pl.when(group < other)
        def _():
            pl.semaphore_wait(ready_sems.at[other], 1)
            onward(other).start()
    for other in range(groups - 1):
        @pl.when(group > other)
        def _():
            upstream(other).wait_recv()

    total = land3[0].astype(f32)
    for other in range(1, groups - 1):
        total = total + land3[other].astype(f32)
    for source in range(heads):
        send2[source] = total.astype(bf16)
        total = total + land1[source].astype(f32)
    for step in order:
        exchange(*second, step).start()
    land2[member] = send2[member]
    ones = jnp.full((HDIM, HDIM), 1 / HDIM, bf16)

    def add_prefix(head, place):
        prefix = land2[head].astype(f32)
        for chunk in range(chunks):
            outputs = inner[head, chunk] + jnp.dot(
                q_feat[head, chunk], (prefix + states[chunk, head]).astype(bf16), preferred_element_type=f32
            )
            whole[place % 2][chunk] = outputs
            squares[place % 2][chunk] = (outputs * outputs).astype(bf16)

    def norm(head, place):
        lanes = pl.ds(pl.multiple_of(head * HDIM, HDIM), HDIM)
        gain = g_ref[0:1, lanes]
        for chunk in range(chunks):
            mean = jnp.dot(squares[place % 2][chunk], ones, preferred_element_type=f32)
            scaled = whole[place % 2][chunk] * lax.rsqrt(mean + 1e-06) * gain
            out_ref[pl.ds(chunk * CHUNK, CHUNK), lanes] = scaled.astype(bf16)

    add_prefix(member, 0)
    norm(member, 0)
    last = None
    for place, step in enumerate(order):
        arrival(*second, step).wait_recv()
        add_prefix(partner(step), place + 1)
        if last is not None:
            norm(last, place)
        last = partner(step)
    norm(last, len(order))

    @pl.when(me < n - 1)
    def _():
        for kind in range(3):
            halo(kind).wait_send()

    for step in order:
        exchange(*first, step).wait_send()
        exchange(*second, step).wait_send()
    for other in range(1, groups):
        @pl.when(group < other)
        def _():
            onward(other).wait_send()


def body(queries, key_rows, value_rows, conv_weight, head_gain):
    tokens, width = queries.shape
    heads = width // HDIM
    n = lax.axis_size("ctx")
    groups = n // heads
    chunks = tokens // CHUNK
    bf16, f32 = jnp.bfloat16, jnp.float32
    dma = pltpu.SemaphoreType.DMA
    operands = (queries, key_rows, value_rows, conv_weight, head_gain.reshape(1, width))
    return pl.pallas_call(
        functools.partial(kernel, n, heads, tokens),
        out_shape=jax.ShapeDtypeStruct((tokens, width), bf16),
        in_specs=[pl.BlockSpec(memory_space=pltpu.HBM)] * 5,
        out_specs=pl.BlockSpec(memory_space=pltpu.VMEM),
        scratch_shapes=[
            *[pltpu.VMEM((tokens + PAD, width), bf16)] * 3,
            *[pltpu.VMEM((TAIL, width), bf16)] * 2,
            pltpu.VMEM((3, CONV, width), f32),
            pltpu.VMEM((1, width), f32),
            *[pltpu.VMEM((heads, chunks, CHUNK, HDIM), bf16)] * 3,
            pltpu.VMEM((heads, chunks, CHUNK, HDIM), f32),
            pltpu.VMEM((chunks, heads, HDIM, HDIM), f32),
            *[pltpu.VMEM((chunks, CHUNK, HDIM), f32)] * 2,
            *[pltpu.VMEM((chunks, CHUNK, HDIM), bf16)] * 2,
            *[pltpu.VMEM((heads, HDIM, HDIM), bf16)] * 4,
            pltpu.VMEM((HDIM, HDIM), bf16),
            pltpu.VMEM((groups - 1, HDIM, HDIM), bf16),
            pltpu.VMEM((2 * heads, CHUNK + PAD, HDIM), f32),
            dma((4, chunks)), dma((3,)), dma((3,)),
            dma((heads,)), dma((heads,)), dma((heads,)), dma((heads,)), dma((groups,)), dma((groups,)),
            pltpu.SemaphoreType.REGULAR((groups,)),
        ],
        compiler_params=pltpu.CompilerParams(
            collective_id=0, has_side_effects=True, vmem_limit_bytes=48 * 1024 * 1024
        ),
        name="linear_attention",
    )(*[pltpu.with_memory_space_constraint(x, pltpu.HBM) for x in operands])


def solution(mesh):
    return jax.shard_map(
        body,
        mesh=mesh,
        in_specs=(
            P(("mp", "ctx"), None),
            P(("mp", "ctx"), None),
            P(("mp", "ctx"), None),
            P("mp", None, None),
            P("mp"),
        ),
        out_specs=P(("mp", "ctx"), None),
        check_vma=False,
    )
```
